32 devices in a mesh: dp: 4 (over y, x), seq: 8 (over z, core).
Axes of the slice: x: 2, y: 2, z: 4, core: 2. Of those that a mesh axis runs over, the one named last changes fastest.
Arguments:
- hidden_in: bfloat16 [8, 1024, 1536], P('dp', 'seq'), may hold values from -6 to 6
- lengths: int32 [8], P('dp'), may hold values from 256 to 1024, as said below
- cotangent: bfloat16 [8, 1024, 1536], P('dp', 'seq'), may hold values from -6 to 6
- attn_gain: bfloat16 [1536], P(('dp', 'seq')), may hold values from 0.25 to 1.75
- q_weight: bfloat16 [1536, 1536], P(('dp', 'seq')), may hold values from -0.15625 to 0.15625
- q_bias: bfloat16 [1536], P(('dp', 'seq')), may hold values from -3 to 3
- k_weight: bfloat16 [256, 1536], P(('dp', 'seq')), may hold values from -0.15625 to 0.15625
- k_bias: bfloat16 [256], P(('dp', 'seq')), may hold values from -3 to 3
- v_weight: bfloat16 [256, 1536], P(('dp', 'seq')), may hold values from -0.15625 to 0.15625
- v_bias: bfloat16 [256], P(('dp', 'seq')), may hold values from -0.59765625 to 0.59765625
- o_weight: bfloat16 [1536, 1536], P(('dp', 'seq')), may hold values from -0.875 to 0.875
- mlp_gain: bfloat16 [1536], P(('dp', 'seq')), may hold values from 0.25 to 1.75
- gate_weight: bfloat16 [8960, 1536], P(('dp', 'seq')), may hold values from -0.15625 to 0.15625
- up_weight: bfloat16 [8960, 1536], P(('dp', 'seq')), may hold values from -0.15625 to 0.15625
- down_weight: bfloat16 [1536, 8960], P(None, ('dp', 'seq')), may hold values from -0.0625 to 0.0625
Outputs:
- block_out: bfloat16 [8, 1024, 1536], P('dp', 'seq')
- input_grad: float32 [8, 1024, 1536], P('dp', 'seq')
- attn_gain_grad: float32 [1536], P(('dp', 'seq'))
- q_weight_grad: float32 [1536, 1536], P(('dp', 'seq'))
- q_bias_grad: float32 [1536], P(('dp', 'seq'))
- k_weight_grad: float32 [256, 1536], P(('dp', 'seq'))
- k_bias_grad: float32 [256], P(('dp', 'seq'))
- v_weight_grad: float32 [256, 1536], P(('dp', 'seq'))
- v_bias_grad: float32 [256], P(('dp', 'seq'))
- o_weight_grad: float32 [1536, 1536], P(('dp', 'seq'))
- mlp_gain_grad: float32 [1536], P(('dp', 'seq'))
- gate_weight_grad: float32 [8960, 1536], P(('dp', 'seq'))
- up_weight_grad: float32 [8960, 1536], P(('dp', 'seq'))
- down_weight_grad: float32 [1536, 8960], P(None, ('dp', 'seq'))
The draws below stay inside these ranges and needn't reach their ends.
Inputs may be any that keep to these rules, and one draw needn't show every extreme that they name: Slots t < lengths[b] of sequence b are valid; in every draw at least one sequence is valid in all 1024 slots.
All inputs are finite; a program needn't handle non-finite values.
Results may differ from the reference program's by a relative error of at most 0.025.
Values may be sent and summed in bfloat16 or wider, within the bound.
No kernel may reach another device: no remote copies, remote signals or barrier semaphores. Data moves between devices by JAX's collectives and lax.ppermute only.
A program may use at most 448 MiB of HBM per device.

```python
import math
import jax
import jax.numpy as jnp
from jax import lax

D = 1536
HEADS = 12
KV_HEADS = 2
HEAD = 128
FF = 8960
KVD = 256
SEQ_LEN = 1024
SEQS = 8
QB = 512


def draw_lengths(key, part):
    drawn = jax.random.randint(key, (SEQS,), SEQ_LEN // 4, SEQ_LEN + 1)
    full_index = jax.random.randint(jax.random.fold_in(key, 7), (), 0, SEQS)
    return jnp.where(jnp.arange(SEQS) == full_index, SEQ_LEN, drawn).astype(jnp.int32)


def block_levels(key, dims, pieces, low, largest):
    factor_of = 1.0
    for axis_at, shards_of in pieces:
        steps = jax.random.uniform(jax.random.fold_in(jax.random.fold_in(key, 6), axis_at), (shards_of,), jnp.float32, low / len(pieces), largest / len(pieces))
        factor_of = factor_of * jnp.repeat(jnp.exp(steps), dims[axis_at] // shards_of).reshape((-1,) + (1,) * (len(dims) - 1 - axis_at))
    return factor_of


def bell_draw(rng, dims, spread, most, shards=(), held_as=jnp.bfloat16):
    values = jax.random.normal(rng, dims, jnp.float32) * spread
    if len(shards) > 0:
        values = block_levels(rng, dims, shards, -0.22, 0.18) * values
    return jnp.clip(values, min=-most, max=most).astype(held_as)


def setup_inputs(seed: int = 0) -> dict:
    key_list = jax.random.split(jax.random.key(seed), 16)
    return {
        "hidden_in": bell_draw(key_list[0], (SEQS, SEQ_LEN, D), 1.0, 6.0, ((0, 4), (1, 8))),
        "lengths": draw_lengths(jax.random.fold_in(key_list[15], 71), 0),
        "cotangent": bell_draw(key_list[2], (SEQS, SEQ_LEN, D), 1.0, 6.0, ((0, 4), (1, 8))),
        "attn_gain": jnp.clip(1.0 + 0.15 * jax.random.normal(key_list[3], (D,), jnp.float32), 0.25, 1.75).astype(jnp.bfloat16),
        "q_weight": bell_draw(key_list[4], (D, D), D ** -0.5, 0.15625, ((0, 32),)),
        "q_bias": bell_draw(key_list[5], (D,), 0.5, 3.0, ((0, 32),)),
        "k_weight": bell_draw(key_list[6], (KVD, D), D ** -0.5, 0.15625, ((0, 32),)),
        "k_bias": bell_draw(key_list[7], (KVD,), 0.5, 3.0, ((0, 32),)),
        "v_weight": bell_draw(key_list[8], (KVD, D), D ** -0.5, 0.15625, ((0, 32),)),
        "v_bias": bell_draw(key_list[9], (KVD,), 0.1, 0.59765625, ((0, 32),)),
        "o_weight": bell_draw(key_list[10], (D, D), (D // 32) ** -0.5, 0.875, ((0, 32),)),
        "mlp_gain": jnp.clip(1.0 + 0.15 * jax.random.normal(key_list[11], (D,), jnp.float32), 0.25, 1.75).astype(jnp.bfloat16),
        "gate_weight": bell_draw(key_list[12], (FF, D), D ** -0.5, 0.15625, ((0, 32),)),
        "up_weight": bell_draw(key_list[13], (FF, D), D ** -0.5, 0.15625, ((0, 32),)),
        "down_weight": bell_draw(key_list[14], (D, FF), FF ** -0.5, 0.0625, ((1, 32),)),
    }


EPSILON = 1e-06
NEGATIVE = -1e+30
HIGHEST = lax.Precision.HIGHEST

@jax.custom_vjp
def low(v):
    return lax.optimization_barrier(v.astype(jnp.bfloat16)).astype(jnp.float32)

@jax.custom_vjp
def low_back(v):
    return v

def low_keep(v):
    return (low(v), None)

def low_pass(kept, grad):
    return (grad,)

def back_keep(v):
    return (v, None)

def back_low(kept, grad):
    return (low(grad),)
low.defvjp(low_keep, low_pass)
low_back.defvjp(back_keep, back_low)

def matmul_high(left_side, right_side):
    return jnp.dot(left_side, right_side, precision=HIGHEST)

def rms_norm(values, gain_values):
    return values * lax.rsqrt(lax.optimization_barrier(jnp.mean(values * values, axis=-1, keepdims=True)) + EPSILON) * gain_values

def rope_tables(positions):
    half_size = HEAD // 2
    inverse = jnp.exp(-math.log(1000000.0) * 2.0 * jnp.arange(half_size).astype(jnp.float32) / HEAD)
    angles = positions[:, None] * inverse[None, :]
    angles = jnp.concatenate([angles, angles], axis=1)
    return (jnp.cos(angles), jnp.sin(angles))

def rotate(values, cosine, sine_table):
    half_size = HEAD // 2
    turned = jnp.concatenate([-values[..., half_size:], values[..., :half_size]], axis=-1)
    return values * cosine[:, None, :] + turned * sine_table[:, None, :]

def attend_block(query_block, block_start, key_heads, value_heads):
    query_pos = block_start + jnp.arange(query_block.shape[0]).astype(jnp.int32)
    key_pos = jnp.arange(key_heads.shape[0]).astype(jnp.int32)
    causal = query_pos[:, None] >= key_pos[None, :]
    scores = jnp.einsum('qkgd,skd->kgqs', query_block, key_heads, precision=HIGHEST) * (1.0 / math.sqrt(HEAD))
    scores = low_back(scores)
    scores = jnp.where(causal[None, None], scores, NEGATIVE)
    row_top = lax.optimization_barrier(jnp.max(scores, axis=-1, keepdims=True))
    exponent = jnp.exp(scores - row_top)
    soft_probs = low(exponent / lax.optimization_barrier(jnp.sum(exponent, axis=-1, keepdims=True)))
    return jnp.einsum('kgqs,skd->qkgd', soft_probs, value_heads, precision=HIGHEST)

def one_sequence(inputs, valid_length, params):
    attn_gain, q_weight, q_bias, k_weight, k_bias, v_weight, v_bias, o_weight, mlp_gain, gate_weight, up_weight, down_weight = params
    seq_rows = inputs.shape[0]
    attn_in = low(rms_norm(inputs, attn_gain))
    query_lin = low_back(matmul_high(attn_in, q_weight.T) + q_bias)
    key_lin = low_back(matmul_high(attn_in, k_weight.T) + k_bias)
    value_lin = low_back(matmul_high(attn_in, v_weight.T) + v_bias)
    cosine, sine_table = rope_tables(jnp.arange(seq_rows).astype(jnp.float32))
    query_heads = low(rotate(query_lin.reshape(seq_rows, HEADS, HEAD), cosine, sine_table))
    key_heads = low(rotate(key_lin.reshape(seq_rows, KV_HEADS, HEAD), cosine, sine_table))
    value_heads = low(value_lin).reshape(seq_rows, KV_HEADS, HEAD)
    block_count = seq_rows // QB
    query_blocks = query_heads.reshape(block_count, QB, KV_HEADS, HEADS // KV_HEADS, HEAD)
    block_starts = (jnp.arange(block_count) * QB).astype(jnp.int32)
    blockwise = jax.checkpoint(lambda block_pair: attend_block(block_pair[0], block_pair[1], key_heads, value_heads))
    mixed_heads = lax.map(blockwise, (query_blocks, block_starts)).reshape(seq_rows, D)
    mixed_low = low(low_back(mixed_heads))
    resid = inputs + low_back(matmul_high(mixed_low, o_weight.T))
    mlp_in = low(rms_norm(resid, mlp_gain))
    gate_lin = low_back(matmul_high(mlp_in, gate_weight.T))
    up_lin = low_back(matmul_high(mlp_in, up_weight.T))
    hidden_low = low(gate_lin * jax.nn.sigmoid(gate_lin) * up_lin)
    result = resid + low_back(matmul_high(hidden_low, down_weight.T))
    valid_rows = jnp.arange(seq_rows).astype(jnp.int32) < valid_length
    return jnp.where(valid_rows[:, None], result, 0.0)

def reference(hidden_in, lengths, cotangent, attn_gain, q_weight, q_bias, k_weight, k_bias, v_weight, v_bias, o_weight, mlp_gain, gate_weight, up_weight, down_weight):
    params = tuple((array_item.astype(jnp.float32) for array_item in (attn_gain, q_weight, q_bias, k_weight, k_bias, v_weight, v_bias, o_weight, mlp_gain, gate_weight, up_weight, down_weight)))
    inputs = hidden_in.astype(jnp.float32)

    def forward(all_inputs, all_params):
        per_sequence = jax.checkpoint(lambda seq_pair: one_sequence(seq_pair[0], seq_pair[1], all_params))
        return lax.map(per_sequence, (all_inputs, lengths))
    result, pullback = jax.vjp(forward, inputs, params)
    input_grad, param_grads = pullback(cotangent.astype(jnp.float32))
    return (result.astype(jnp.bfloat16), input_grad, param_grads[0], param_grads[1], param_grads[2], param_grads[3], param_grads[4], param_grads[5], param_grads[6], param_grads[7], param_grads[8], param_grads[9], param_grads[10], param_grads[11])
```

```python
import math

import jax
import jax.numpy as jnp
from jax import lax
from jax.sharding import PartitionSpec as P

HEADS = 12
KV_HEADS = 2
HEAD = 128


EPSILON = 1e-06
NEGATIVE = -1e30


def times_transposed(left_side, right_side):
    return lax.dot_general(
        left_side, right_side, (((1,), (1,)), ((), ())), preferred_element_type=jnp.float32
    )


def plain_product(left_side, right_side):
    return jnp.dot(left_side, right_side, preferred_element_type=jnp.float32)


def rope_tables(positions):
    half_size = HEAD // 2
    inverse = jnp.exp(-math.log(1000000.0) * 2.0 * jnp.arange(half_size).astype(jnp.float32) / HEAD)
    angles = positions[:, None] * inverse[None, :]
    angles = jnp.concatenate([angles, angles], axis=1)
    return (jnp.cos(angles), jnp.sin(angles))


def rotate(values, cosine, sine_table):
    half_size = HEAD // 2
    turned = jnp.concatenate([-values[..., half_size:], values[..., :half_size]], axis=-1)
    return values * cosine[:, None, :] + turned * sine_table[:, None, :]


def rotate_back(gradient, cosine, sine_table):
    half_size = HEAD // 2
    scaled = gradient * sine_table[:, None, :]
    turned = jnp.concatenate([scaled[..., half_size:], -scaled[..., :half_size]], axis=-1)
    return gradient * cosine[:, None, :] + turned


def rms_parts(values):
    inverse = lax.rsqrt(jnp.mean(values * values, axis=-1, keepdims=True) + EPSILON)
    return (values * inverse, inverse)


def rms_back(upstream, normal_values, inverse, gain_values):
    scaled = upstream * gain_values
    gain_grad = jnp.sum(upstream * normal_values, axis=0)
    input_part = inverse * (
        scaled - normal_values * jnp.mean(scaled * normal_values, axis=-1, keepdims=True)
    )
    return (input_part, gain_grad)


def masked_scores(query_heads, key_heads, causal, score_scale):
    scores = (
        jnp.einsum("qkgd,skd->kgqs", query_heads, key_heads, preferred_element_type=jnp.float32)
        * score_scale
    )
    return jnp.where(causal[None, None], scores, NEGATIVE)


def weight_grad(columns, inputs_all):
    return lax.dot_general(
        columns, inputs_all, (((0,), (0,)), ((), ())), preferred_element_type=jnp.float32
    ).astype(jnp.bfloat16)


def column_sum(columns):
    return jnp.sum(columns.astype(jnp.float32), axis=0)


ALL = ("dp", "seq")


def swap(values, axis, bit):
    size = lax.axis_size(axis)
    return lax.ppermute(values, axis, [(index, index ^ bit) for index in range(size)])


def gather_dp(block):
    if lax.axis_size("dp") != 4:
        return lax.all_gather(block, "dp", axis=0, tiled=True)
    half = block.shape[1] // 2
    from_x = swap(block, "dp", 1)
    from_y = swap(block, "dp", 2)
    corner = jnp.concatenate(
        [swap(from_x[:, :half], "dp", 2), swap(from_y[:, half:], "dp", 1)], axis=1
    )
    return jnp.concatenate([block, from_x, from_y, corner], axis=0)


def add_low(left_side, right_side):
    total = left_side.astype(jnp.float32) + right_side.astype(jnp.float32)
    return total.astype(jnp.bfloat16)


def scatter_dp(grads):
    if lax.axis_size("dp") != 4:
        return lax.psum_scatter(grads, "dp", scatter_dimension=0, tiled=True).astype(jnp.float32)
    m = grads.shape[0] // 4
    half = grads.shape[1] // 2
    own, to_x, to_y, corner = (grads[i * m : (i + 1) * m] for i in range(4))
    via_x = swap(corner[:, :half], "dp", 1)
    via_y = swap(corner[:, half:], "dp", 2)
    to_y = jnp.concatenate([add_low(to_y[:, :half], via_x), to_y[:, half:]], axis=1)
    to_x = jnp.concatenate([to_x[:, :half], add_low(to_x[:, half:], via_y)], axis=1)
    got_x = swap(to_x, "dp", 1)
    got_y = swap(to_y, "dp", 2)
    return own.astype(jnp.float32) + got_x.astype(jnp.float32) + got_y.astype(jnp.float32)


def pack_rows(pieces, width):
    flat = jnp.concatenate(pieces)
    return jnp.pad(flat, (0, 8 * width - flat.shape[0])).reshape(8, width)


def unpack_rows(rows, sizes):
    flat = rows.reshape(rows.shape[0], -1)
    parts, at = [], 0
    for size in sizes:
        parts.append(flat[:, at : at + size].reshape(-1))
        at += size
    return parts


def gather_seq(block):
    return lax.all_gather(block, "seq", axis=0, tiled=True)


def scatter_seq(parts):
    return lax.psum_scatter(parts, "seq", scatter_dimension=0, tiled=True).astype(jnp.float32)


def on_device(
    hidden_in,
    lengths,
    cotangent,
    attn_gain,
    q_weight,
    q_bias,
    k_weight,
    k_bias,
    v_weight,
    v_bias,
    o_weight,
    mlp_gain,
    gate_weight,
    up_weight,
    down_weight,
):
    micro_count, span_rows, model_width = hidden_in.shape
    rows = micro_count * span_rows
    full_len = span_rows * lax.axis_size("seq")
    shards = lax.axis_size("dp") * lax.axis_size("seq")
    group_share = HEADS // KV_HEADS
    kv_width = KV_HEADS * HEAD
    score_scale = 1.0 / math.sqrt(HEAD)
    positions = lax.axis_index("seq") * span_rows + jnp.arange(span_rows, dtype=jnp.int32)
    cosine, sine_table = rope_tables(positions.astype(jnp.float32))
    causal = positions[:, None] >= jnp.arange(full_len, dtype=jnp.int32)[None, :]
    q_rows, k_rows, units = q_weight.shape[0], k_weight.shape[0], gate_weight.shape[0]
    small_sizes = (q_rows, q_rows, q_rows, k_rows, k_rows)

    small = pack_rows((attn_gain, mlp_gain, q_bias, k_bias, v_bias), model_width)
    attn_block = jnp.concatenate([q_weight, k_weight, v_weight, small], axis=0)
    attn_all = lax.all_gather(attn_block, ALL, axis=0, tiled=False)
    cuts = (0, q_rows, q_rows + k_rows, q_rows + 2 * k_rows)
    query_w = attn_all[:, cuts[0] : cuts[1]].reshape(-1, model_width)
    key_w = attn_all[:, cuts[1] : cuts[2]].reshape(-1, model_width)
    value_w = attn_all[:, cuts[2] : cuts[3]].reshape(-1, model_width)
    gain_one, gain_two, query_b, key_b, value_b = (
        piece.astype(jnp.float32) for piece in unpack_rows(attn_all[:, cuts[3] :], small_sizes)
    )
    output_w = lax.all_gather(o_weight, ALL, axis=0, tiled=True)

    valid_rows = (positions[None, :] < lengths[:, None]).reshape(rows)
    upstream_low = jnp.where(valid_rows[:, None], cotangent.reshape(rows, model_width), 0)
    upstream = upstream_low.astype(jnp.float32)
    upstream_all = gather_seq(upstream_low)
    gate_w, up_w, down_w = (
        gather_dp(gate_weight),
        gather_dp(up_weight),
        gather_dp(down_weight.T),
    )

    inputs = hidden_in.reshape(rows, model_width).astype(jnp.float32)
    normal_one, inverse_one = rms_parts(inputs)
    attn_in = (normal_one * gain_one).astype(jnp.bfloat16)
    query_lin = times_transposed(attn_in, query_w) + query_b
    key_lin = times_transposed(attn_in, key_w) + key_b
    value_lin = times_transposed(attn_in, value_w) + value_b
    query_rot = rotate(
        query_lin.reshape(micro_count, span_rows, HEADS, HEAD), cosine, sine_table
    ).astype(jnp.bfloat16)
    key_rot = (
        rotate(key_lin.reshape(micro_count, span_rows, KV_HEADS, HEAD), cosine, sine_table)
        .astype(jnp.bfloat16)
        .reshape(micro_count, span_rows, kv_width)
    )
    value_low = value_lin.astype(jnp.bfloat16).reshape(micro_count, span_rows, kv_width)
    pair_all = lax.all_gather(
        jnp.concatenate([key_rot, value_low], axis=-1), "seq", axis=1, tiled=True
    )
    key_all, value_all = pair_all[..., :kv_width], pair_all[..., kv_width:]
    query_heads = query_rot.reshape(micro_count, span_rows, KV_HEADS, group_share, HEAD)
    key_heads = key_all.reshape(micro_count, full_len, KV_HEADS, HEAD)
    value_heads = value_all.reshape(micro_count, full_len, KV_HEADS, HEAD)
    mixed_parts = []
    log_parts = []
    for batch_index in range(micro_count):
        scores = masked_scores(
            query_heads[batch_index], key_heads[batch_index], causal, score_scale
        )
        row_top = jnp.max(scores, axis=-1, keepdims=True)
        exponent = jnp.exp(scores - row_top)
        row_total = jnp.sum(exponent, axis=-1, keepdims=True)
        log_parts.append(row_top + jnp.log(row_total))
        soft_low = (exponent / row_total).astype(jnp.bfloat16)
        mixed_heads = jnp.einsum(
            "kgqs,skd->qkgd", soft_low, value_heads[batch_index], preferred_element_type=jnp.float32
        )
        mixed_parts.append(mixed_heads.reshape(span_rows, model_width))
    mixed_low = jnp.concatenate(mixed_parts, axis=0).astype(jnp.bfloat16)
    resid = inputs + times_transposed(mixed_low, output_w)
    normal_two, inverse_two = rms_parts(resid)
    mlp_in = (normal_two * gain_two).astype(jnp.bfloat16)

    mlp_all = gather_seq(mlp_in)
    gate_lin = times_transposed(mlp_all, gate_w)
    up_lin = times_transposed(mlp_all, up_w)
    hidden_grad = times_transposed(upstream_all, down_w)
    gate_sigma = jax.nn.sigmoid(gate_lin)
    hidden_low = (gate_lin * gate_sigma * up_lin).astype(jnp.bfloat16)
    gate_grad = (
        hidden_grad * up_lin * (gate_sigma * (1.0 + gate_lin * (1.0 - gate_sigma)))
    ).astype(jnp.bfloat16)
    up_grad = (hidden_grad * gate_lin * gate_sigma).astype(jnp.bfloat16)
    mlp_part = plain_product(gate_grad, gate_w) + plain_product(up_grad, up_w)
    mlp_in_grad = scatter_seq(mlp_part.astype(jnp.bfloat16))
    result = resid + scatter_seq(plain_product(hidden_low, down_w).astype(jnp.bfloat16))
    block_out = (
        jnp.where(valid_rows[:, None], result, 0.0)
        .astype(jnp.bfloat16)
        .reshape(micro_count, span_rows, model_width)
    )
    gate_w_grad, up_w_grad, down_w_grad = (
        scatter_dp(weight_grad(gate_grad, mlp_all)),
        scatter_dp(weight_grad(up_grad, mlp_all)),
        scatter_dp(weight_grad(hidden_low, upstream_all)).T,
    )

    norm_two_grad, gain_two_grad = rms_back(mlp_in_grad, normal_two, inverse_two, gain_two)
    resid_grad = upstream + norm_two_grad
    resid_low = resid_grad.astype(jnp.bfloat16)
    output_part = weight_grad(resid_low, mixed_low)
    output_w_grad = lax.psum_scatter(output_part, ALL, scatter_dimension=0, tiled=True).astype(
        jnp.float32
    )
    mixed_grad = (
        plain_product(resid_low, output_w)
        .astype(jnp.bfloat16)
        .reshape(micro_count, span_rows, KV_HEADS, group_share, HEAD)
    )
    query_parts = []
    key_parts = []
    value_parts = []
    for batch_index in range(micro_count):
        again_scores = masked_scores(
            query_heads[batch_index], key_heads[batch_index], causal, score_scale
        )
        soft_probs = jnp.exp(again_scores - log_parts[batch_index])
        probs_low = soft_probs.astype(jnp.bfloat16)
        prob_grad = jnp.einsum(
            "qkgd,skd->kgqs",
            mixed_grad[batch_index],
            value_heads[batch_index],
            preferred_element_type=jnp.float32,
        )
        value_all_grad = jnp.einsum(
            "kgqs,qkgd->skd", probs_low, mixed_grad[batch_index], preferred_element_type=jnp.float32
        )
        row_delta = jnp.sum(soft_probs * prob_grad, axis=-1, keepdims=True)
        score_grad = (soft_probs * (prob_grad - row_delta)).astype(jnp.bfloat16)
        query_parts.append(
            jnp.einsum(
                "kgqs,skd->qkgd",
                score_grad,
                key_heads[batch_index],
                preferred_element_type=jnp.float32,
            )
            * score_scale
        )
        key_parts.append(
            (
                jnp.einsum(
                    "kgqs,qkgd->skd",
                    score_grad,
                    query_heads[batch_index],
                    preferred_element_type=jnp.float32,
                )
                * score_scale
            ).reshape(full_len, kv_width)
        )
        value_parts.append(value_all_grad.reshape(full_len, kv_width))
    pair_grad = lax.psum_scatter(
        jnp.concatenate([jnp.stack(key_parts), jnp.stack(value_parts)], axis=-1).astype(
            jnp.bfloat16
        ),
        "seq",
        scatter_dimension=1,
        tiled=True,
    ).astype(jnp.float32)
    key_grad, value_grad = pair_grad[..., :kv_width], pair_grad[..., kv_width:]
    query_grad = jnp.stack(query_parts).reshape(micro_count, span_rows, HEADS, HEAD)
    query_low = (
        rotate_back(query_grad, cosine, sine_table).reshape(rows, model_width).astype(jnp.bfloat16)
    )
    key_low = (
        rotate_back(key_grad.reshape(micro_count, span_rows, KV_HEADS, HEAD), cosine, sine_table)
        .reshape(rows, kv_width)
        .astype(jnp.bfloat16)
    )
    value_grad_low = value_grad.reshape(rows, kv_width).astype(jnp.bfloat16)
    attn_in_grad = (
        plain_product(query_low, query_w)
        + plain_product(key_low, key_w)
        + plain_product(value_grad_low, value_w)
    )
    norm_one_grad, gain_one_grad = rms_back(attn_in_grad, normal_one, inverse_one, gain_one)
    input_grad = (resid_grad + norm_one_grad).reshape(micro_count, span_rows, model_width)
    small_grads = jnp.concatenate(
        [
            piece.reshape(shards, -1)
            for piece in (
                gain_one_grad,
                gain_two_grad,
                column_sum(query_low),
                column_sum(key_low),
                column_sum(value_grad_low),
            )
        ],
        axis=1,
    ).astype(jnp.bfloat16)
    small_grads = jnp.pad(
        small_grads, ((0, 0), (0, 8 * model_width - small_grads.shape[1]))
    ).reshape(shards, 8, model_width)
    grad_block = jnp.concatenate(
        [
            weight_grad(query_low, attn_in).reshape(shards, q_rows, model_width),
            weight_grad(key_low, attn_in).reshape(shards, k_rows, model_width),
            weight_grad(value_grad_low, attn_in).reshape(shards, k_rows, model_width),
            small_grads,
        ],
        axis=1,
    )
    totals = (
        lax.psum_scatter(
            grad_block.reshape(-1, model_width), ALL, scatter_dimension=0, tiled=True
        )
        .astype(jnp.float32)
    )
    small_totals = unpack_rows(totals[None, cuts[3] :], small_sizes)
    return (
        block_out,
        input_grad,
        small_totals[0],
        totals[cuts[0] : cuts[1]],
        small_totals[2],
        totals[cuts[1] : cuts[2]],
        small_totals[3],
        totals[cuts[2] : cuts[3]],
        small_totals[4],
        output_w_grad,
        small_totals[1],
        gate_w_grad,
        up_w_grad,
        down_w_grad,
    )


def solution(mesh):
    placed = (
        P("dp", "seq", None),
        P("dp"),
        P("dp", "seq", None),
        P(("dp", "seq")),
        P(("dp", "seq"), None),
        P(("dp", "seq")),
        P(("dp", "seq"), None),
        P(("dp", "seq")),
        P(("dp", "seq"), None),
        P(("dp", "seq")),
        P(("dp", "seq"), None),
        P(("dp", "seq")),
        P(("dp", "seq"), None),
        P(("dp", "seq"), None),
        P(None, ("dp", "seq")),
    )
    return jax.shard_map(
        on_device,
        mesh=mesh,
        in_specs=placed,
        out_specs=(
            P("dp", "seq", None),
            P("dp", "seq", None),
            P(("dp", "seq")),
            P(("dp", "seq"), None),
            P(("dp", "seq")),
            P(("dp", "seq"), None),
            P(("dp", "seq")),
            P(("dp", "seq"), None),
            P(("dp", "seq")),
            P(("dp", "seq"), None),
            P(("dp", "seq")),
            P(("dp", "seq"), None),
            P(("dp", "seq"), None),
            P(None, ("dp", "seq")),
        ),
        check_vma=False,
    )
```

```python
import functools
import math

import jax
import jax.numpy as jnp
from jax import lax
from jax.experimental import pallas as pl
from jax.experimental.pallas import tpu as pltpu
from jax.sharding import PartitionSpec as P

HEADS = 12
KV_HEADS = 2
HEAD = 128


EPSILON = 1e-06
NEGATIVE = -1e30


def times_transposed(left_side, right_side):
    return lax.dot_general(
        left_side, right_side, (((1,), (1,)), ((), ())), preferred_element_type=jnp.float32
    )


def plain_product(left_side, right_side):
    return jnp.dot(left_side, right_side, preferred_element_type=jnp.float32)


def rope_tables(positions):
    half_size = HEAD // 2
    inverse = jnp.exp(-math.log(1000000.0) * 2.0 * jnp.arange(half_size).astype(jnp.float32) / HEAD)
    angles = positions[:, None] * inverse[None, :]
    angles = jnp.concatenate([angles, angles], axis=1)
    return (jnp.cos(angles), jnp.sin(angles))


def rotate(values, cosine, sine_table):
    half_size = HEAD // 2
    turned = jnp.concatenate([-values[..., half_size:], values[..., :half_size]], axis=-1)
    return values * cosine[:, None, :] + turned * sine_table[:, None, :]


def rotate_back(gradient, cosine, sine_table):
    half_size = HEAD // 2
    scaled = gradient * sine_table[:, None, :]
    turned = jnp.concatenate([scaled[..., half_size:], -scaled[..., :half_size]], axis=-1)
    return gradient * cosine[:, None, :] + turned


def rms_parts(values):
    inverse = lax.rsqrt(jnp.mean(values * values, axis=-1, keepdims=True) + EPSILON)
    return (values * inverse, inverse)


def rms_back(upstream, normal_values, inverse, gain_values):
    scaled = upstream * gain_values
    gain_grad = jnp.sum(upstream * normal_values, axis=0)
    input_part = inverse * (
        scaled - normal_values * jnp.mean(scaled * normal_values, axis=-1, keepdims=True)
    )
    return (input_part, gain_grad)


def masked_scores(query_heads, key_heads, causal, score_scale):
    scores = (
        jnp.einsum("qkgd,skd->kgqs", query_heads, key_heads, preferred_element_type=jnp.float32)
        * score_scale
    )
    return jnp.where(causal[None, None], scores, NEGATIVE)


def weight_grad(columns, inputs_all):
    return lax.dot_general(
        columns, inputs_all, (((0,), (0,)), ((), ())), preferred_element_type=jnp.float32
    ).astype(jnp.bfloat16)


def column_sum(columns):
    return jnp.sum(columns.astype(jnp.float32), axis=0)


ALL = ("dp", "seq")


def swap(values, axis, bit):
    size = lax.axis_size(axis)
    return lax.ppermute(values, axis, [(index, index ^ bit) for index in range(size)])


def gather_dp(block):
    return lax.all_gather(block, "dp", axis=0, tiled=True)


def add_low(left_side, right_side):
    total = left_side.astype(jnp.float32) + right_side.astype(jnp.float32)
    return total.astype(jnp.bfloat16)


def scatter_dp(grads):
    return lax.psum_scatter(grads, "dp", scatter_dimension=0, tiled=True).astype(jnp.float32)


def pack_rows(pieces, width):
    flat = jnp.concatenate(pieces)
    return jnp.pad(flat, (0, 8 * width - flat.shape[0])).reshape(8, width)


def unpack_rows(rows, sizes):
    flat = rows.reshape(rows.shape[0], -1)
    parts, at = [], 0
    for size in sizes:
        parts.append(flat[:, at : at + size].reshape(-1))
        at += size
    return parts


def gather_seq(block):
    return lax.all_gather(block, "seq", axis=0, tiled=True)


def scatter_seq(parts):
    return lax.psum_scatter(parts, "seq", scatter_dimension=0, tiled=True).astype(jnp.float32)


def on_any_mesh(
    hidden_in,
    lengths,
    cotangent,
    attn_gain,
    q_weight,
    q_bias,
    k_weight,
    k_bias,
    v_weight,
    v_bias,
    o_weight,
    mlp_gain,
    gate_weight,
    up_weight,
    down_weight,
):
    micro_count, span_rows, model_width = hidden_in.shape
    rows = micro_count * span_rows
    full_len = span_rows * lax.axis_size("seq")
    shards = lax.axis_size("dp") * lax.axis_size("seq")
    group_share = HEADS // KV_HEADS
    kv_width = KV_HEADS * HEAD
    score_scale = 1.0 / math.sqrt(HEAD)
    positions = lax.axis_index("seq") * span_rows + jnp.arange(span_rows, dtype=jnp.int32)
    cosine, sine_table = rope_tables(positions.astype(jnp.float32))
    causal = positions[:, None] >= jnp.arange(full_len, dtype=jnp.int32)[None, :]
    q_rows, k_rows, units = q_weight.shape[0], k_weight.shape[0], gate_weight.shape[0]
    small_sizes = (q_rows, q_rows, q_rows, k_rows, k_rows)

    small = pack_rows((attn_gain, mlp_gain, q_bias, k_bias, v_bias), model_width)
    attn_block = jnp.concatenate([q_weight, k_weight, v_weight, small], axis=0)
    attn_all = lax.all_gather(attn_block, ALL, axis=0, tiled=False)
    cuts = (0, q_rows, q_rows + k_rows, q_rows + 2 * k_rows)
    query_w = attn_all[:, cuts[0] : cuts[1]].reshape(-1, model_width)
    key_w = attn_all[:, cuts[1] : cuts[2]].reshape(-1, model_width)
    value_w = attn_all[:, cuts[2] : cuts[3]].reshape(-1, model_width)
    gain_one, gain_two, query_b, key_b, value_b = (
        piece.astype(jnp.float32) for piece in unpack_rows(attn_all[:, cuts[3] :], small_sizes)
    )
    output_w = lax.all_gather(o_weight, ALL, axis=0, tiled=True)

    valid_rows = (positions[None, :] < lengths[:, None]).reshape(rows)
    upstream_low = jnp.where(valid_rows[:, None], cotangent.reshape(rows, model_width), 0)
    upstream = upstream_low.astype(jnp.float32)
    upstream_all = gather_seq(upstream_low)
    gate_w, up_w, down_w = (
        gather_dp(gate_weight),
        gather_dp(up_weight),
        gather_dp(down_weight.T),
    )

    inputs = hidden_in.reshape(rows, model_width).astype(jnp.float32)
    normal_one, inverse_one = rms_parts(inputs)
    attn_in = (normal_one * gain_one).astype(jnp.bfloat16)
    query_lin = times_transposed(attn_in, query_w) + query_b
    key_lin = times_transposed(attn_in, key_w) + key_b
    value_lin = times_transposed(attn_in, value_w) + value_b
    query_rot = rotate(
        query_lin.reshape(micro_count, span_rows, HEADS, HEAD), cosine, sine_table
    ).astype(jnp.bfloat16)
    key_rot = (
        rotate(key_lin.reshape(micro_count, span_rows, KV_HEADS, HEAD), cosine, sine_table)
        .astype(jnp.bfloat16)
        .reshape(micro_count, span_rows, kv_width)
    )
    value_low = value_lin.astype(jnp.bfloat16).reshape(micro_count, span_rows, kv_width)
    pair_all = lax.all_gather(
        jnp.concatenate([key_rot, value_low], axis=-1), "seq", axis=1, tiled=True
    )
    key_all, value_all = pair_all[..., :kv_width], pair_all[..., kv_width:]
    query_heads = query_rot.reshape(micro_count, span_rows, KV_HEADS, group_share, HEAD)
    key_heads = key_all.reshape(micro_count, full_len, KV_HEADS, HEAD)
    value_heads = value_all.reshape(micro_count, full_len, KV_HEADS, HEAD)
    mixed_parts = []
    log_parts = []
    for batch_index in range(micro_count):
        scores = masked_scores(
            query_heads[batch_index], key_heads[batch_index], causal, score_scale
        )
        row_top = jnp.max(scores, axis=-1, keepdims=True)
        exponent = jnp.exp(scores - row_top)
        row_total = jnp.sum(exponent, axis=-1, keepdims=True)
        log_parts.append(row_top + jnp.log(row_total))
        soft_low = (exponent / row_total).astype(jnp.bfloat16)
        mixed_heads = jnp.einsum(
            "kgqs,skd->qkgd", soft_low, value_heads[batch_index], preferred_element_type=jnp.float32
        )
        mixed_parts.append(mixed_heads.reshape(span_rows, model_width))
    mixed_low = jnp.concatenate(mixed_parts, axis=0).astype(jnp.bfloat16)
    resid = inputs + times_transposed(mixed_low, output_w)
    normal_two, inverse_two = rms_parts(resid)
    mlp_in = (normal_two * gain_two).astype(jnp.bfloat16)

    mlp_all = gather_seq(mlp_in)
    gate_lin = times_transposed(mlp_all, gate_w)
    up_lin = times_transposed(mlp_all, up_w)
    hidden_grad = times_transposed(upstream_all, down_w)
    gate_sigma = jax.nn.sigmoid(gate_lin)
    hidden_low = (gate_lin * gate_sigma * up_lin).astype(jnp.bfloat16)
    gate_grad = (
        hidden_grad * up_lin * (gate_sigma * (1.0 + gate_lin * (1.0 - gate_sigma)))
    ).astype(jnp.bfloat16)
    up_grad = (hidden_grad * gate_lin * gate_sigma).astype(jnp.bfloat16)
    mlp_part = plain_product(gate_grad, gate_w) + plain_product(up_grad, up_w)
    mlp_in_grad = scatter_seq(mlp_part.astype(jnp.bfloat16))
    result = resid + scatter_seq(plain_product(hidden_low, down_w).astype(jnp.bfloat16))
    block_out = (
        jnp.where(valid_rows[:, None], result, 0.0)
        .astype(jnp.bfloat16)
        .reshape(micro_count, span_rows, model_width)
    )
    gate_w_grad, up_w_grad, down_w_grad = (
        scatter_dp(weight_grad(gate_grad, mlp_all)),
        scatter_dp(weight_grad(up_grad, mlp_all)),
        scatter_dp(weight_grad(hidden_low, upstream_all)).T,
    )

    norm_two_grad, gain_two_grad = rms_back(mlp_in_grad, normal_two, inverse_two, gain_two)
    resid_grad = upstream + norm_two_grad
    resid_low = resid_grad.astype(jnp.bfloat16)
    output_part = weight_grad(resid_low, mixed_low)
    output_w_grad = lax.psum_scatter(output_part, ALL, scatter_dimension=0, tiled=True).astype(
        jnp.float32
    )
    mixed_grad = (
        plain_product(resid_low, output_w)
        .astype(jnp.bfloat16)
        .reshape(micro_count, span_rows, KV_HEADS, group_share, HEAD)
    )
    query_parts = []
    key_parts = []
    value_parts = []
    for batch_index in range(micro_count):
        again_scores = masked_scores(
            query_heads[batch_index], key_heads[batch_index], causal, score_scale
        )
        soft_probs = jnp.exp(again_scores - log_parts[batch_index])
        probs_low = soft_probs.astype(jnp.bfloat16)
        prob_grad = jnp.einsum(
            "qkgd,skd->kgqs",
            mixed_grad[batch_index],
            value_heads[batch_index],
            preferred_element_type=jnp.float32,
        )
        value_all_grad = jnp.einsum(
            "kgqs,qkgd->skd", probs_low, mixed_grad[batch_index], preferred_element_type=jnp.float32
        )
        row_delta = jnp.sum(soft_probs * prob_grad, axis=-1, keepdims=True)
        score_grad = (soft_probs * (prob_grad - row_delta)).astype(jnp.bfloat16)
        query_parts.append(
            jnp.einsum(
                "kgqs,skd->qkgd",
                score_grad,
                key_heads[batch_index],
                preferred_element_type=jnp.float32,
            )
            * score_scale
        )
        key_parts.append(
            (
                jnp.einsum(
                    "kgqs,qkgd->skd",
                    score_grad,
                    query_heads[batch_index],
                    preferred_element_type=jnp.float32,
                )
                * score_scale
            ).reshape(full_len, kv_width)
        )
        value_parts.append(value_all_grad.reshape(full_len, kv_width))
    pair_grad = lax.psum_scatter(
        jnp.concatenate([jnp.stack(key_parts), jnp.stack(value_parts)], axis=-1).astype(
            jnp.bfloat16
        ),
        "seq",
        scatter_dimension=1,
        tiled=True,
    ).astype(jnp.float32)
    key_grad, value_grad = pair_grad[..., :kv_width], pair_grad[..., kv_width:]
    query_grad = jnp.stack(query_parts).reshape(micro_count, span_rows, HEADS, HEAD)
    query_low = (
        rotate_back(query_grad, cosine, sine_table).reshape(rows, model_width).astype(jnp.bfloat16)
    )
    key_low = (
        rotate_back(key_grad.reshape(micro_count, span_rows, KV_HEADS, HEAD), cosine, sine_table)
        .reshape(rows, kv_width)
        .astype(jnp.bfloat16)
    )
    value_grad_low = value_grad.reshape(rows, kv_width).astype(jnp.bfloat16)
    attn_in_grad = (
        plain_product(query_low, query_w)
        + plain_product(key_low, key_w)
        + plain_product(value_grad_low, value_w)
    )
    norm_one_grad, gain_one_grad = rms_back(attn_in_grad, normal_one, inverse_one, gain_one)
    input_grad = (resid_grad + norm_one_grad).reshape(micro_count, span_rows, model_width)
    small_grads = jnp.concatenate(
        [
            piece.reshape(shards, -1)
            for piece in (
                gain_one_grad,
                gain_two_grad,
                column_sum(query_low),
                column_sum(key_low),
                column_sum(value_grad_low),
            )
        ],
        axis=1,
    ).astype(jnp.bfloat16)
    small_grads = jnp.pad(
        small_grads, ((0, 0), (0, 8 * model_width - small_grads.shape[1]))
    ).reshape(shards, 8, model_width)
    grad_block = jnp.concatenate(
        [
            weight_grad(query_low, attn_in).reshape(shards, q_rows, model_width),
            weight_grad(key_low, attn_in).reshape(shards, k_rows, model_width),
            weight_grad(value_grad_low, attn_in).reshape(shards, k_rows, model_width),
            small_grads,
        ],
        axis=1,
    )
    totals = (
        lax.psum_scatter(
            grad_block.reshape(-1, model_width), ALL, scatter_dimension=0, tiled=True
        )
        .astype(jnp.float32)
    )
    small_totals = unpack_rows(totals[None, cuts[3] :], small_sizes)
    return (
        block_out,
        input_grad,
        small_totals[0],
        totals[cuts[0] : cuts[1]],
        small_totals[2],
        totals[cuts[1] : cuts[2]],
        small_totals[3],
        totals[cuts[2] : cuts[3]],
        small_totals[4],
        output_w_grad,
        small_totals[1],
        gate_w_grad,
        up_w_grad,
        down_w_grad,
    )


def sync(*values):
    return lax.optimization_barrier(values)


def hop(values, moves):
    pairs = [(2 * a + core, 2 * b + core) for a, b in moves for core in range(2)]
    return lax.ppermute(values, "seq", pairs)


def other_core(values):
    return swap(values, "seq", 1)


def chip_is(*chips):
    place = lax.axis_index("seq") // 2
    return functools.reduce(jnp.logical_or, [place == chip for chip in chips])


UP = ((0, 1), (1, 2), (2, 3))
DOWN = ((3, 2), (2, 1), (1, 0))
ARRIVALS = ((0, 1, 2, 3), (1, 2, 0, 3), (2, 1, 3, 0), (3, 2, 1, 0))


def line_one(block):
    return hop(block, UP), hop(block, DOWN)


def line_two(one):
    return hop(one[0], UP[1:]), hop(one[1], DOWN[1:])


def line_middle(two):
    return jnp.where(chip_is(2, 3), two[0], two[1])


def line_three(middle):
    return hop(middle, ((2, 3), (1, 0)))


def line_slot_one(one):
    return jnp.where(chip_is(0, 1), one[1], one[0])


def line_slot_two(one, middle):
    return jnp.where(chip_is(0, 3), middle, jnp.where(chip_is(1), one[0], one[1]))


def line_slot_three(middle, third):
    return jnp.where(chip_is(0, 3), third, middle)


def sum_one(parts):
    return hop(parts[3], ((0, 1), (3, 2)))


def sum_two(parts, first):
    value = jnp.where(chip_is(0, 3), parts[2], add_low(parts[3], first))
    return hop(value, UP[:2]), hop(value, DOWN[:2])


def sum_three(parts, second):
    up = add_low(jnp.where(chip_is(2), parts[2], parts[1]), second[0])
    down = add_low(jnp.where(chip_is(1), parts[2], parts[1]), second[1])
    return hop(up, UP), hop(down, DOWN)


def sum_done(parts, third):
    return sum(part.astype(jnp.float32) for part in (parts[0], *third))


def square_one(block):
    return swap(block, "dp", 1), swap(block, "dp", 2)


def square_two(one):
    half = one[0].shape[-1] // 2
    return swap(one[0][..., :half], "dp", 2), swap(one[1][..., half:], "dp", 1)


def square_pieces(block, one, two):
    return [block, one[0], one[1], jnp.concatenate(two, axis=-1)]


def back_one(parts):
    half = parts[0].shape[-1] // 2
    return swap(parts[3][..., :half], "dp", 1), swap(parts[3][..., half:], "dp", 2)


def back_two(parts, one):
    half = parts[0].shape[-1] // 2
    to_x = jnp.concatenate([parts[1][..., :half], add_low(parts[1][..., half:], one[1])], axis=-1)
    to_y = jnp.concatenate([add_low(parts[2][..., :half], one[0]), parts[2][..., half:]], axis=-1)
    return swap(to_x, "dp", 1), swap(to_y, "dp", 2)


def back_done(parts, two):
    return sum(part.astype(jnp.float32) for part in (parts[0], *two))


def join_cores(part):
    return add_low(part[0], other_core(part[1]))


def shard_index():
    here, group = lax.axis_index("seq"), lax.axis_index("dp")
    place, core = here // 2, here % 2
    chips = jnp.array(ARRIVALS, jnp.int32)[place]
    four, two = jnp.arange(4, dtype=jnp.int32), jnp.arange(2, dtype=jnp.int32)
    to_relative = (
        (four[None, :, None] ^ group) * 8 + chips[None, None, :] * 2 + (two[:, None, None] ^ core)
    ).reshape(-1)
    return chips, to_relative


SCALE = 1.0 / math.sqrt(HEAD)
SHARE = HEADS // KV_HEADS
NT = (((1,), (1,)), ((), ()))
NN = (((1,), (0,)), ((), ()))
TN = (((0,), (0,)), ((), ()))


def dot_low(left_side, right_side, dims):
    return lax.dot_general(left_side, right_side, dims, preferred_element_type=jnp.float32)


def turn(values, cosine, signed_sine):
    return values * cosine + pltpu.roll(values, HEAD // 2, 1) * signed_sine


def turn_back(values, cosine, signed_sine):
    return values * cosine - pltpu.roll(values, HEAD // 2, 1) * signed_sine


def pair_kernel(inputs_ref, key_ref, value_ref, kb_ref, vb_ref, cos_ref, sin_ref, out_ref):
    linear = dot_low(inputs_ref[...], key_ref[...], NT) + kb_ref[...]
    for head in range(KV_HEADS):
        at = slice(head * HEAD, (head + 1) * HEAD)
        out_ref[:, at] = turn(linear[:, at], cos_ref[...], sin_ref[...]).astype(jnp.bfloat16)
    rest = slice(KV_HEADS * HEAD, None)
    linear = dot_low(inputs_ref[...], value_ref[...], NT) + vb_ref[...]
    out_ref[:, rest] = linear.astype(jnp.bfloat16)


def project_pair(attn_in, key_w, value_w, key_b, value_b, cosine, signed_sine):
    rows, copies = attn_in.shape[0], attn_in.shape[0] // cosine.shape[0]
    return pl.pallas_call(
        pair_kernel, out_shape=jax.ShapeDtypeStruct((rows, 2 * key_w.shape[0]), jnp.bfloat16)
    )(
        attn_in,
        key_w,
        value_w,
        key_b.reshape(1, -1),
        value_b.reshape(1, -1),
        jnp.tile(cosine, (copies, 1)),
        jnp.tile(signed_sine, (copies, 1)),
    )


def allowed(meta_ref, part, span, width):
    key = lax.broadcasted_iota(jnp.int32, (span, width), 0)
    query = lax.broadcasted_iota(jnp.int32, (span, width), 1) % span
    return key + (meta_ref[1 + part] - meta_ref[0]) * span <= query


def attend_kernel(
    meta_ref, q_ref, k_ref, v_ref, cos_ref, sin_ref, low_ref, out_ref, log_ref, heads_ref, s_ref
):
    parts, span = k_ref.shape[0], k_ref.shape[1]
    width = SHARE * span
    for head in range(SHARE):
        at = slice(head * HEAD, (head + 1) * HEAD)
        rotated = turn(q_ref[:, at], cos_ref[...], sin_ref[...]).astype(jnp.bfloat16)
        low_ref[:, at] = rotated
        heads_ref[head * span : (head + 1) * span, :] = rotated
    top = jnp.full((1, width), NEGATIVE, jnp.float32)
    for part in range(parts):
        scores = dot_low(k_ref[part], heads_ref[...], NT) * SCALE
        scores = jnp.where(allowed(meta_ref, part, span, width), scores, NEGATIVE)
        s_ref[part] = scores
        top = jnp.maximum(top, jnp.max(scores, axis=0, keepdims=True))
    total = jnp.zeros((1, width), jnp.float32)
    for part in range(parts):
        exponent = jnp.exp(s_ref[part] - top)
        s_ref[part] = exponent
        total = total + jnp.sum(exponent, axis=0, keepdims=True)
    share = 1.0 / total
    mixed = jnp.zeros((HEAD, width), jnp.float32)
    for part in range(parts):
        mixed = mixed + dot_low(v_ref[part], (s_ref[part] * share).astype(jnp.bfloat16), TN)
    for head in range(SHARE):
        out_ref[:, head * HEAD : (head + 1) * HEAD] = (
            mixed[:, head * span : (head + 1) * span].T.astype(jnp.bfloat16)
        )
    log_ref[...] = jnp.broadcast_to(top + jnp.log(total), log_ref.shape[1:])[None]


def attention_specs(rows, span, parts):
    group = SHARE * HEAD
    return {
        "queries": pl.BlockSpec((span, group), lambda b, j, *_: (b, j)),
        "keys": pl.BlockSpec((parts, span, HEAD), lambda b, j, *_: (0, b, j)),
        "values": pl.BlockSpec((parts, span, HEAD), lambda b, j, *_: (0, b, KV_HEADS + j)),
        "table": pl.BlockSpec((span, HEAD), lambda b, j, *_: (0, 0)),
        "logs": pl.BlockSpec((1, 8, SHARE * span), lambda b, j, *_: (b * KV_HEADS + j, 0, 0)),
    }


def attend(query_lin, pair_all, meta, cosine, signed_sine):
    rows, width = query_lin.shape
    span, parts = cosine.shape[0], pair_all.shape[0]
    batch = rows // span
    spec = attention_specs(rows, span, parts)
    return pl.pallas_call(
        attend_kernel,
        grid_spec=pltpu.PrefetchScalarGridSpec(
            num_scalar_prefetch=1,
            grid=(batch, KV_HEADS),
            in_specs=[
                spec["queries"],
                spec["keys"],
                spec["values"],
                spec["table"],
                spec["table"],
            ],
            out_specs=[spec["queries"], spec["queries"], spec["logs"]],
            scratch_shapes=[
                pltpu.VMEM((SHARE * span, HEAD), jnp.bfloat16),
                pltpu.VMEM((parts, span, SHARE * span), jnp.float32),
            ],
        ),
        out_shape=[
            jax.ShapeDtypeStruct((rows, width), jnp.bfloat16),
            jax.ShapeDtypeStruct((rows, width), jnp.bfloat16),
            jax.ShapeDtypeStruct((batch * KV_HEADS, 8, SHARE * span), jnp.float32),
        ],
    )(meta, query_lin, pair_all, pair_all, cosine, signed_sine)


def attend_back_kernel(
    meta_ref,
    low_ref,
    up_ref,
    k_ref,
    v_ref,
    log_ref,
    cos_ref,
    sin_ref,
    dq_ref,
    dpair_ref,
    heads_ref,
    ups_ref,
    p_ref,
    d_ref,
):
    parts, span = k_ref.shape[0], k_ref.shape[1]
    width = SHARE * span
    for head in range(SHARE):
        at = slice(head * HEAD, (head + 1) * HEAD)
        heads_ref[head * span : (head + 1) * span, :] = low_ref[:, at]
        ups_ref[head * span : (head + 1) * span, :] = up_ref[:, at]
    logs = log_ref[0, 0:1, :]
    delta = jnp.zeros((1, width), jnp.float32)
    group = pl.program_id(1)

    def put(part, first, values):
        for index in range(KV_HEADS):

            @pl.when(group == index)
            def _():
                at = (first + index) * HEAD
                dpair_ref[part, :, at : at + HEAD] = values.astype(jnp.bfloat16)

    for part in range(parts):
        scores = dot_low(k_ref[part], heads_ref[...], NT) * SCALE
        probs = jnp.where(
            allowed(meta_ref, part, span, width), jnp.exp(jnp.minimum(scores - logs, 0.0)), 0.0
        )
        prob_grad = dot_low(v_ref[part], ups_ref[...], NT)
        p_ref[part] = probs
        d_ref[part] = prob_grad
        delta = delta + jnp.sum(probs * prob_grad, axis=0, keepdims=True)
        put(part, KV_HEADS, dot_low(probs.astype(jnp.bfloat16), ups_ref[...], NN))
    dq = jnp.zeros((HEAD, width), jnp.float32)
    for part in range(parts):
        score_grad = (p_ref[part] * (d_ref[part] - delta)).astype(jnp.bfloat16)
        put(part, 0, dot_low(score_grad, heads_ref[...], NN) * SCALE)
        dq = dq + dot_low(k_ref[part], score_grad, TN)
    for head in range(SHARE):
        gradient = dq[:, head * span : (head + 1) * span].T * SCALE
        dq_ref[:, head * HEAD : (head + 1) * HEAD] = turn_back(
            gradient, cos_ref[...], sin_ref[...]
        ).astype(jnp.bfloat16)


def attend_back(query_low, pair_all, mixed_grad, logs, meta, cosine, signed_sine):
    rows, width = query_low.shape
    span, parts = cosine.shape[0], pair_all.shape[0]
    spec = attention_specs(rows, span, parts)
    return pl.pallas_call(
        attend_back_kernel,
        grid_spec=pltpu.PrefetchScalarGridSpec(
            num_scalar_prefetch=1,
            grid=(rows // span, KV_HEADS),
            in_specs=[
                spec["queries"],
                spec["queries"],
                spec["keys"],
                spec["values"],
                spec["logs"],
                spec["table"],
                spec["table"],
            ],
            out_specs=[
                spec["queries"],
                pl.BlockSpec((parts, span, pair_all.shape[2]), lambda b, j, *_: (0, b, 0)),
            ],
            scratch_shapes=[
                pltpu.VMEM((SHARE * span, HEAD), jnp.bfloat16),
                pltpu.VMEM((SHARE * span, HEAD), jnp.bfloat16),
                pltpu.VMEM((parts, span, SHARE * span), jnp.float32),
                pltpu.VMEM((parts, span, SHARE * span), jnp.float32),
            ],
        ),
        out_shape=[
            jax.ShapeDtypeStruct((rows, width), jnp.bfloat16),
            jax.ShapeDtypeStruct(pair_all.shape, jnp.bfloat16),
        ],
    )(meta, query_low, mixed_grad, pair_all, pair_all, logs, cosine, signed_sine)


def feed_kernel(*refs):
    x_refs, y_refs, gate_ref, up_ref, down_ref = refs[0:2], refs[2:4], refs[4], refs[5], refs[6]
    hidden_ref, dgate_ref, dup_ref, in_ref, back_ref = refs[-9:-4]
    grad_refs, out_refs = refs[-4:-2], refs[-2:]
    m = x_refs[0].shape[0]
    for half in range(2):
        at = slice(half * m, (half + 1) * m)
        x, y = x_refs[half][...], y_refs[half][...]
        in_ref[at, :] = x
        back_ref[at, :] = y
        gate = dot_low(x, gate_ref[...], NT)
        up = dot_low(x, up_ref[...], NT)
        grad = dot_low(y, down_ref[...], NT)
        sigma = jax.nn.sigmoid(gate)
        swish = gate * sigma
        hidden = (swish * up).astype(jnp.bfloat16)
        dgate = (grad * up * (sigma * (1.0 + gate * (1.0 - sigma)))).astype(jnp.bfloat16)
        dup = (grad * swish).astype(jnp.bfloat16)
        hidden_ref[at, :] = hidden
        dgate_ref[at, :] = dgate
        dup_ref[at, :] = dup
        grad_refs[half][...] = (
            dot_low(dgate, gate_ref[...], NN) + dot_low(dup, up_ref[...], NN)
        ).astype(jnp.bfloat16)
        out_refs[half][...] = dot_low(hidden, down_ref[...], NN).astype(jnp.bfloat16)


def feed_forward(rows_in, rows_back, weights, slot, slots, kept):
    m, width = rows_in[0].shape
    units = weights[0].shape[0]
    whole = pl.BlockSpec((m, width), lambda i: (0, 0))
    weight = pl.BlockSpec((units, width), lambda i: (0, 0))
    high = [pl.BlockSpec((2 * m, n), lambda i: (slot, 0)) for n in (units,) * 3 + (width,) * 2]
    wide = [
        jax.ShapeDtypeStruct((slots * 2 * m, n), jnp.bfloat16) for n in (units,) * 3 + (width,) * 2
    ]
    low = [jax.ShapeDtypeStruct((m, width), jnp.bfloat16)] * 4
    kept = list(kept or ())
    results = pl.pallas_call(
        feed_kernel,
        grid=(1,),
        in_specs=[whole] * 4 + [weight] * 3 + [pl.BlockSpec(memory_space=pl.ANY)] * len(kept),
        out_specs=high + [whole] * 4,
        out_shape=wide + low,
        input_output_aliases={7 + i: i for i in range(len(kept))},
    )(*rows_in, *rows_back, *weights, *kept)
    return results[:5], results[5:7], results[7:9]


def place_kernel(order_ref, *refs):
    count = (len(refs) - 3) or 1
    sources, mine, theirs, sem = refs[:count], refs[count], refs[count + 1], refs[count + 2]
    blocks = mine.shape[0]
    copies = []
    for index in range(2 * blocks):
        target = mine if index < blocks else theirs
        at = 0
        for source in sources:
            m = source.shape[1]
            copies.append(
                pltpu.make_async_copy(
                    source.at[order_ref[index]],
                    target.at[index % blocks, pl.ds(at, m)],
                    sem.at[len(copies)],
                )
            )
            at += m
    for copy in copies:
        copy.start()
    for copy in copies:
        copy.wait()


def split_square(sources, to_relative):
    shards, _, w = sources[0].shape
    total = sum(source.shape[1] for source in sources)
    shape = jax.ShapeDtypeStruct((shards // 2, total, w), jnp.bfloat16)
    anywhere = pl.BlockSpec(memory_space=pl.ANY)
    mine, theirs = pl.pallas_call(
        place_kernel,
        grid_spec=pltpu.PrefetchScalarGridSpec(
            num_scalar_prefetch=1,
            grid=(1,),
            in_specs=[pl.BlockSpec(memory_space=pltpu.VMEM)] * len(sources),
            out_specs=[anywhere] * 2,
            scratch_shapes=[pltpu.SemaphoreType.DMA((shards * len(sources),))],
        ),
        out_shape=[shape, shape],
    )(to_relative, *sources)
    return tuple(part.reshape(4, -1, w) for part in (mine, theirs))


def cut_kernel(cuts, source, *refs):
    outs, sem = refs[:-1], refs[-1]
    copies = []
    for index in range(source.shape[0]):
        for out, (low, high) in zip(outs, cuts):
            m = high - low
            copies.append(
                pltpu.make_async_copy(
                    source.at[index, pl.ds(low, m)],
                    out.at[pl.ds(index * m, m)],
                    sem.at[len(copies)],
                )
            )
    for copy in copies:
        copy.start()
    for copy in copies:
        copy.wait()


def cut_rows(source, cuts):
    blocks, _, w = source.shape
    anywhere = pl.BlockSpec(memory_space=pl.ANY)
    return pl.pallas_call(
        functools.partial(cut_kernel, cuts),
        in_specs=[pl.BlockSpec(memory_space=pltpu.VMEM)],
        out_specs=[anywhere] * len(cuts),
        out_shape=[
            jax.ShapeDtypeStruct((blocks * (high - low), w), jnp.bfloat16) for low, high in cuts
        ],
        scratch_shapes=[pltpu.SemaphoreType.DMA((blocks * len(cuts),))],
    )(source)


def on_device(
    hidden_in,
    lengths,
    cotangent,
    attn_gain,
    q_weight,
    q_bias,
    k_weight,
    k_bias,
    v_weight,
    v_bias,
    o_weight,
    mlp_gain,
    gate_weight,
    up_weight,
    down_weight,
):
    micro_count, span_rows, model_width = hidden_in.shape
    rows = micro_count * span_rows
    kv_width = KV_HEADS * HEAD
    here = lax.axis_index("seq")
    positions = here * span_rows + jnp.arange(span_rows, dtype=jnp.int32)
    cosine, sine_table = rope_tables(positions.astype(jnp.float32))
    half_signs = jnp.where(jnp.arange(HEAD) < HEAD // 2, -1.0, 1.0)
    signed_sine = sine_table * half_signs[None, :]
    q_rows, k_rows, units = q_weight.shape[0], k_weight.shape[0], gate_weight.shape[0]
    small_sizes = (q_rows, q_rows, q_rows, k_rows, k_rows)
    chips, to_relative = shard_index()
    spans = 2 * chips[:, None] + (jnp.arange(2, dtype=jnp.int32)[None, :] ^ (here % 2))
    meta = jnp.concatenate([here[None], spans.reshape(-1)])
    table = (meta, cosine, signed_sine)

    small = pack_rows((attn_gain, mlp_gain, q_bias, k_bias, v_bias), model_width)
    attn_block = jnp.concatenate([q_weight, o_weight, k_weight, v_weight, small], axis=0)
    mlp_block = jnp.concatenate([gate_weight, up_weight, down_weight.T], axis=0)
    attn_all = lax.all_gather(attn_block, ALL, axis=0, tiled=False)
    mlp_one = square_one(mlp_block)
    inputs = hidden_in.reshape(rows, model_width).astype(jnp.float32)
    normal_one, inverse_one = rms_parts(inputs)
    valid_rows = (positions[None, :] < lengths[:, None]).reshape(rows)
    upstream_low = jnp.where(valid_rows[:, None], cotangent.reshape(rows, model_width), 0)
    upstream = upstream_low.astype(jnp.float32)
    attn_all, mlp_one, upstream_low, normal_one = sync(
        attn_all, mlp_one, upstream_low, normal_one
    )
    at = 2 * q_rows
    key_w, value_w, query_w = cut_rows(
        attn_all, ((at, at + k_rows), (at + k_rows, at + 2 * k_rows), (0, q_rows))
    )
    gain_one, gain_two, query_b, key_b, value_b = (
        piece.astype(jnp.float32)
        for piece in unpack_rows(attn_all[:, at + 2 * k_rows :], small_sizes)
    )
    attn_in = (normal_one * gain_one).astype(jnp.bfloat16)
    pair = project_pair(attn_in, key_w, value_w, key_b, value_b, cosine, signed_sine)

    one = line_one(pair)
    query_lin = times_transposed(attn_in, query_w) + query_b
    one, query_lin, upstream_low = sync(one, query_lin, upstream_low)
    two = line_two(one)
    upstream_one = line_one(upstream_low)
    mlp_two = square_two(mlp_one)
    (output_w,) = cut_rows(attn_all, ((q_rows, at),))
    two, output_w = sync(two, output_w)
    middle = line_middle(two)
    third = line_three(middle)
    (third,) = sync(third)
    pair_all = jnp.stack(
        [
            pair,
            line_slot_one(one),
            line_slot_two(one, middle),
            line_slot_three(middle, third),
        ]
    )
    pair_all = jnp.stack([pair_all, other_core(pair_all)], axis=1)
    pair_all = pair_all.reshape(-1, rows, 2 * kv_width)
    pair_all, upstream_one = sync(pair_all, upstream_one)
    upstream_two = line_two(upstream_one)
    query_low, mixed_low, logs = attend(query_lin, pair_all, *table)
    mixed_low, mlp_two, upstream_two = sync(mixed_low, mlp_two, upstream_two)
    upstream_middle = line_middle(upstream_two)
    upstream_three = line_three(upstream_middle)
    resid = inputs + times_transposed(mixed_low, output_w)
    normal_two, inverse_two = rms_parts(resid)
    mlp_in = (normal_two * gain_two).astype(jnp.bfloat16)

    (mlp_in,) = sync(mlp_in)
    one = line_one(mlp_in)
    mlp_pieces = square_pieces(mlp_block, mlp_one, mlp_two)
    weights = [
        jnp.concatenate([piece[i * units : (i + 1) * units] for piece in mlp_pieces], axis=0)
        for i in range(3)
    ]

    def slot(index, mine, upstream_part, kept):
        return feed_forward(
            (mine, other_core(mine)),
            (upstream_part, other_core(upstream_part)),
            weights,
            index,
            4,
            kept,
        )

    kept, grad_zero, out_zero = slot(0, mlp_in, upstream_low, None)
    one, kept, upstream_three = sync(one, kept, upstream_three)
    two = line_two(one)
    kept, grad_one, out_one = slot(1, line_slot_one(one), line_slot_one(upstream_one), kept)
    two, kept = sync(two, kept)
    middle = line_middle(two)
    third = line_three(middle)
    kept, grad_two, out_two = slot(
        2, line_slot_two(one, middle), line_slot_two(upstream_one, upstream_middle), kept
    )
    third, kept = sync(third, kept)
    kept, grad_three, out_three = slot(
        3, line_slot_three(middle, third), line_slot_three(upstream_middle, upstream_three), kept
    )
    mlp_parts = [join_cores(part) for part in (grad_zero, grad_one, grad_two, grad_three)]
    mlp_parts, kept = sync(mlp_parts, kept)
    hidden_all, gate_all, up_all, mlp_all, upstream_all = kept
    first = sum_one(mlp_parts)
    gate_grad = weight_grad(gate_all, mlp_all)
    first, gate_grad = sync(first, gate_grad)
    second = sum_two(mlp_parts, first)
    up_grad = weight_grad(up_all, mlp_all)
    wide_grads = [
        jnp.concatenate([g[i * units : (i + 1) * units] for g in (gate_grad, up_grad)], axis=0)
        for i in range(4)
    ]
    second, wide_grads = sync(second, wide_grads)
    mlp_third = sum_three(mlp_parts, second)
    wide_back = back_one(wide_grads)
    down_grad = weight_grad(hidden_all, upstream_all)
    out_parts = [join_cores(part) for part in (out_zero, out_one, out_two, out_three)]
    mlp_third, down_grad, wide_back, out_parts = sync(
        mlp_third, down_grad, wide_back, out_parts
    )
    mlp_in_grad = sum_done(mlp_parts, mlp_third)

    wide_last = back_two(wide_grads, wide_back)
    out_first = sum_one(out_parts)
    norm_two_grad, gain_two_grad = rms_back(mlp_in_grad, normal_two, inverse_two, gain_two)
    resid_grad = upstream + norm_two_grad
    resid_low = resid_grad.astype(jnp.bfloat16)
    mixed_grad = plain_product(resid_low, output_w).astype(jnp.bfloat16)
    query_grad, pair_parts = attend_back(query_low, pair_all, mixed_grad, logs, *table)
    query_grad, pair_parts, out_first = sync(query_grad, pair_parts, out_first)
    pair_parts = pair_parts.reshape(4, 2, rows, 2 * kv_width)
    pair_mine = add_low(pair_parts[:, 0], other_core(pair_parts[:, 1]))
    first = sum_one(pair_mine)
    out_second = sum_two(out_parts, out_first)
    query_part = weight_grad(query_grad, attn_in).reshape(-1, q_rows, model_width)
    output_part = weight_grad(resid_low, mixed_low).reshape(-1, q_rows, model_width)
    mine, theirs = split_square((query_part, output_part), to_relative)
    first, mine, theirs, wide_last = sync(first, mine, theirs, wide_last)
    second = sum_two(pair_mine, first)
    got = other_core(theirs)
    down_grads = [down_grad[i * units : (i + 1) * units] for i in range(4)]
    down_back = back_one(down_grads)
    second, got = sync(second, got)
    third = sum_three(pair_mine, second)
    wide_mine = add_low(mine, got)
    attn_back = back_one(wide_mine)
    attn_in_grad = plain_product(query_grad, query_w)
    third, attn_back, attn_in_grad, down_back, out_second = sync(
        third, attn_back, attn_in_grad, down_back, out_second
    )
    attn_last = back_two(wide_mine, attn_back)
    out_third = sum_three(out_parts, out_second)
    pair_grad = sum_done(pair_mine, third)
    key_grad, value_grad = pair_grad[:, :kv_width], pair_grad[:, kv_width:]
    key_low = (
        rotate_back(
            key_grad.reshape(micro_count, span_rows, KV_HEADS, HEAD), cosine, sine_table
        )
        .reshape(rows, kv_width)
        .astype(jnp.bfloat16)
    )
    value_grad_low = value_grad.astype(jnp.bfloat16)
    attn_in_grad = (
        attn_in_grad + plain_product(key_low, key_w) + plain_product(value_grad_low, value_w)
    )
    norm_one_grad, gain_one_grad = rms_back(attn_in_grad, normal_one, inverse_one, gain_one)
    shards = 32
    small_grads = jnp.concatenate(
        [
            piece.reshape(shards, -1)
            for piece in (
                gain_one_grad,
                gain_two_grad,
                column_sum(query_grad),
                column_sum(key_low),
                column_sum(value_grad_low),
            )
        ],
        axis=1,
    ).astype(jnp.bfloat16)
    small_grads = jnp.pad(
        small_grads, ((0, 0), (0, 8 * model_width - small_grads.shape[1]))
    ).reshape(shards, 8, model_width)
    key_part = weight_grad(key_low, attn_in).reshape(shards, k_rows, model_width)
    value_part = weight_grad(value_grad_low, attn_in).reshape(shards, k_rows, model_width)
    mine, theirs = split_square((key_part, value_part, small_grads), to_relative)
    (mine, theirs) = sync(mine, theirs)
    got = other_core(theirs)
    input_grad = resid_grad + norm_one_grad
    got, input_grad = sync(got, input_grad)
    pair_mine = add_low(mine, got)
    pair_back = back_one(pair_mine)
    gate_up = back_done(wide_grads, wide_last)
    pair_back, attn_last, gate_up = sync(pair_back, attn_last, gate_up)
    pair_last = back_two(pair_mine, pair_back)
    down_last = back_two(down_grads, down_back)
    wide_line = back_done(wide_mine, attn_last).astype(jnp.bfloat16).reshape(4, -1, model_width)
    pair_last, wide_line = sync(pair_last, wide_line)
    pair_line = back_done(pair_mine, pair_last).astype(jnp.bfloat16).reshape(4, -1, model_width)
    lines = [jnp.concatenate([w, p], axis=0) for w, p in zip(wide_line, pair_line)]
    first = sum_one(lines)
    result = resid + sum_done(out_parts, out_third)
    block_out = jnp.where(valid_rows[:, None], result, 0.0).astype(jnp.bfloat16)
    first, block_out = sync(first, block_out)
    second = sum_two(lines, first)
    second, down_last = sync(second, down_last)
    third = sum_three(lines, second)
    down_w_grad = back_done(down_grads, down_last).T
    third, down_w_grad = sync(third, down_w_grad)
    total = sum_done(lines, third)
    at = 2 * q_rows
    small_totals = unpack_rows(total[None, at + 2 * k_rows :], small_sizes)
    return (
        block_out.reshape(hidden_in.shape),
        input_grad.reshape(hidden_in.shape),
        small_totals[0],
        total[:q_rows],
        small_totals[2],
        total[at : at + k_rows],
        small_totals[3],
        total[at + k_rows : at + 2 * k_rows],
        small_totals[4],
        total[q_rows:at],
        small_totals[1],
        gate_up[:units],
        gate_up[units:],
        down_w_grad,
    )


def solution(mesh):
    placed = (
        P("dp", "seq", None),
        P("dp"),
        P("dp", "seq", None),
        P(("dp", "seq")),
        P(("dp", "seq"), None),
        P(("dp", "seq")),
        P(("dp", "seq"), None),
        P(("dp", "seq")),
        P(("dp", "seq"), None),
        P(("dp", "seq")),
        P(("dp", "seq"), None),
        P(("dp", "seq")),
        P(("dp", "seq"), None),
        P(("dp", "seq"), None),
        P(None, ("dp", "seq")),
    )
    usual = mesh.shape["dp"] == 4 and mesh.shape["seq"] == 8
    return jax.shard_map(
        on_device if usual else on_any_mesh,
        mesh=mesh,
        in_specs=placed,
        out_specs=(
            P("dp", "seq", None),
            P("dp", "seq", None),
            P(("dp", "seq")),
            P(("dp", "seq"), None),
            P(("dp", "seq")),
            P(("dp", "seq"), None),
            P(("dp", "seq")),
            P(("dp", "seq"), None),
            P(("dp", "seq")),
            P(("dp", "seq"), None),
            P(("dp", "seq")),
            P(("dp", "seq"), None),
            P(("dp", "seq"), None),
            P(None, ("dp", "seq")),
        ),
        check_vma=False,
    )
```
